32 devices in a mesh: grp: 2 (over y), ta: 4 (over z), gx: 4 (over x, core).
Axes of the slice: x: 2, y: 2, z: 4, core: 2. Of those that a mesh axis runs over, the one named last changes fastest.
Arguments:
- vectors: bfloat16 [8, 2, 3, 8192, 128], P(('grp', 'ta'), None, None, 'gx'), parts along dimension 0, may hold values from -6 to 6
- peramb: bfloat16 [8, 16, 2, 128, 128], P(('grp', 'ta')), parts along dimension 0, may hold values from -0.5 to 0.5
- momenta: int32 [8, 3], P('grp'), parts along dimension 0, may hold values from -2 to 2, as said below
- sink_mom: int32 [32], P('grp'), parts along dimension 0, may hold values from 0 to 3
- spin_pick: int32 [32], P('grp'), parts along dimension 0, may hold values from 0 to 15
- src_time: int32 [2], P('grp'), parts along dimension 0, may hold values from 0 to 65535
Outputs:
- corr: float32 [8, 16, 2, 128, 128], P(('grp', 'ta'), 'gx'), parts along dimension 0
The draws below stay inside these ranges and needn't reach their ends.
There are 2 independent parts, one for each index of `grp`. The reference program is written for one: setup_inputs(seed, part) draws one part's arguments, and reference() takes and returns one part's arrays. A program takes and returns all parts, laid end to end along the dimension named above; each array names one. Nothing has to cross between parts.
Inputs may be any that keep to these rules, and one draw needn't show every extreme that they name: `momenta`: every component of every momentum is nonzero.
All inputs are finite; a program needn't handle non-finite values.
Results may differ from the reference program's by a relative error of at most 0.0038.
Values sent between devices are 32-bit elements; how exact they have to be, the bound alone decides.
No kernel may reach another device: no remote copies, remote signals or barrier semaphores. Data moves between devices by JAX's collectives and lax.ppermute only.
A program may use at most 64 MiB of HBM per device.

```python
import math
import jax
import jax.numpy as jnp
from jax import lax

RANK = 128
LY = 32
LZ = 32
NMOM = 4
SPIN_BLOCKS = 16
SPINS = 16
NSITES = 8192
NT = 4


def draw_momenta(key, part):
    magnitude = jax.random.randint(jax.random.fold_in(key, 11), (NMOM, 3), 1, 3)
    signed = jax.random.randint(jax.random.fold_in(key, 12), (NMOM, 3), 0, 2) * 2 - 1
    return (magnitude * signed).astype(jnp.int32)


def plant(array, rng, smallest, top_value):
    longest = array.shape.index(max(array.shape))
    spots = []
    for shift in (0, 1):
        where = [jax.random.randint(jax.random.fold_in(rng, axis), (), 0, length) for axis, length in enumerate(array.shape)]
        where[longest] = (where[longest] + shift) % array.shape[longest]
        spots.append(tuple(where))
    return array.at[spots[0]].set(smallest).at[spots[1]].set(top_value)


def level_of(key, shape, split, smallest, top_value):
    def one(position, parts):
        heights = jax.random.uniform(jax.random.fold_in(jax.random.fold_in(key, 6), position), (parts,), jnp.float32, smallest / len(split), top_value / len(split))
        return jnp.repeat(jnp.exp(heights), shape[position] // parts).reshape((-1,) + (1,) * (len(shape) - position - 1))

    loudness = one(*split[0])
    for cut in split[1:]:
        loudness = loudness * one(*cut)
    return loudness


def bell_draw(stream_key, dims, deviation, bound, shards=(), kind=jnp.bfloat16):
    entries = deviation * jax.random.normal(stream_key, dims, jnp.float32)
    if shards:
        entries = entries * level_of(stream_key, dims, shards, -0.22, 0.18)
    return jnp.clip(entries, -bound, bound).astype(kind)


def setup_inputs(seed: int = 0, part: int = 0) -> dict:
    key_of = jax.random.split(jax.random.key(seed), 7)
    own_keys = jax.random.split(jax.random.fold_in(key_of[6], part), 7)
    vectors = bell_draw(own_keys[0], (NT, 2, 3, NSITES, RANK), 1.0, 6.0, ((0, 4), (3, 4)))
    peramb = bell_draw(own_keys[1], (NT, SPIN_BLOCKS, 2, RANK, RANK), RANK ** -0.5, 0.5, ((0, 4),))
    momenta = draw_momenta(jax.random.fold_in(jax.random.fold_in(key_of[6], part), 71), part)
    sink_mom = plant(jax.random.randint(own_keys[3], (SPINS,), 0, NMOM), jax.random.fold_in(own_keys[3], 1), 0, NMOM - 1).astype(jnp.int32)
    spin_pick = plant(jax.random.randint(own_keys[4], (SPINS,), 0, SPIN_BLOCKS), jax.random.fold_in(own_keys[4], 1), 0, SPIN_BLOCKS - 1).astype(jnp.int32)
    src_time = jax.random.randint(own_keys[5], (1,), 0, 65536).astype(jnp.int32)
    return {"vectors": vectors, "peramb": peramb, "momenta": momenta, "sink_mom": sink_mom, "spin_pick": spin_pick, "src_time": src_time}


def phase_angle(momentum, first_x, count, extent_x):
    site_ids = jnp.arange(count, dtype=jnp.int32)
    coord_x = (first_x + site_ids // (LY * LZ)).astype(jnp.int32)
    coord_y = site_ids // LZ % LY
    coord_z = site_ids % LZ
    part_x = jnp.mod(momentum[0] * coord_x, extent_x).astype(jnp.float32) / extent_x
    part_y = jnp.mod(momentum[1] * coord_y, LY).astype(jnp.float32) / LY
    part_z = jnp.mod(momentum[2] * coord_z, LZ).astype(jnp.float32) / LZ
    return 2.0 * math.pi * (part_x + part_y + part_z)

def elemental(vec_re, vec_im, angle, scale):
    cos_part = jnp.cos(angle)[None, :, None]
    sin_part = jnp.sin(angle)[None, :, None]
    real_f = vec_re.astype(jnp.float32)
    imag_f = vec_im.astype(jnp.float32)
    phased_re = real_f * cos_part + imag_f * sin_part
    phased_im = imag_f * cos_part - real_f * sin_part
    upper = jnp.concatenate([phased_re, phased_im], axis=-1)
    lower = jnp.concatenate([phased_im, -phased_re], axis=-1)
    phased = jnp.concatenate([upper, lower], axis=0).astype(jnp.bfloat16)
    total_rows = phased.shape[0] * phased.shape[1]
    phased = phased.reshape(total_rows, -1)
    stacked = jnp.concatenate([vec_re, vec_im], axis=0).reshape(total_rows, -1)
    product = lax.dot_general(stacked, phased, (((0,), (0,)), ((), ())), preferred_element_type=jnp.float32) * scale
    width = vec_re.shape[-1]
    return jnp.stack([product[:, :width], product[:, width:]])

def matmul_high(left, right):
    return jnp.matmul(left, right, precision=lax.Precision.HIGHEST)

def complex_mul(left, right):
    real_part = matmul_high(left[..., 0, :, :], right[..., 0, :, :]) - matmul_high(left[..., 1, :, :], right[..., 1, :, :])
    imag_part = matmul_high(left[..., 0, :, :], right[..., 1, :, :]) + matmul_high(left[..., 1, :, :], right[..., 0, :, :])
    return jnp.stack([real_part, imag_part], axis=-3)

def reference(vectors, peramb, momenta, sink_mom, spin_pick, src_time):
    sites = vectors.shape[3]
    extent_x = sites // (LY * LZ)
    scale = 1.0 / math.sqrt(vectors.shape[2] * sites)
    angles = jnp.stack([phase_angle(momenta[m], 0, sites, extent_x) for m in range(NMOM)])

    def one_slice(vec_slice):
        return jnp.stack([elemental(vec_slice[0], vec_slice[1], angles[m], scale) for m in range(NMOM)])
    elems = lax.map(one_slice, vectors)
    source = elems[jnp.mod(src_time[0], NT).astype(jnp.int32), 0]
    chosen = peramb[:, spin_pick].astype(jnp.float32)
    half_prod = complex_mul(chosen, source)
    sink = elems[:, sink_mom]
    return complex_mul(sink, half_prod) / math.sqrt(RANK)
```

```python
import functools
import math

import jax
import jax.numpy as jnp
from jax import lax
from jax.experimental import pallas as pl
from jax.experimental.pallas import tpu as pltpu
from jax.sharding import PartitionSpec as P

LY = 32
LZ = 32
SUB = 8
PACK = 16


def turn_part(product, extent):
    if extent & (extent - 1) == 0:
        wrapped = jnp.bitwise_and(product, extent - 1)
    else:
        wrapped = jnp.mod(product, extent)
    return wrapped.astype(jnp.float32) / extent


def phase_tables(momenta_ref, m, first_x, sites, extent_x):
    shape = (SUB, sites // SUB)
    site = lax.broadcasted_iota(jnp.int32, shape, 1) * SUB + lax.broadcasted_iota(
        jnp.int32, shape, 0
    )
    coord_x = first_x + site // (LY * LZ)
    coord_y = site // LZ % LY
    coord_z = site % LZ
    turns = (
        turn_part(momenta_ref[m, 0] * coord_x, extent_x)
        + turn_part(momenta_ref[m, 1] * coord_y, LY)
        + turn_part(momenta_ref[m, 2] * coord_z, LZ)
    )
    angle = (2.0 * math.pi) * (turns - jnp.floor(turns + 0.5))
    return jnp.cos(angle), jnp.sin(angle)


def elemental_kernel(
    first, count, extent_x, scale, momenta_ref, place_ref, vec_ref, keep_ref, send_ref,
    left, phased, total
):
    color = pl.program_id(0)
    sites = vec_ref.shape[2]
    rank = vec_ref.shape[3]
    left[:rank] = vec_ref[0, 0].T
    left[rank:] = vec_ref[1, 0].T
    for k in range(count):
        cos_tab, sin_tab = phase_tables(momenta_ref, first + k, place_ref[0], sites, extent_x)
        for i in range(sites // PACK):
            rows = slice(i * PACK, (i + 1) * PACK)
            real = vec_ref[0, 0, rows, :].astype(jnp.float32)
            imag = vec_ref[1, 0, rows, :].astype(jnp.float32)

            def spread(table):
                return jnp.concatenate(
                    [
                        jnp.broadcast_to(table[:, 2 * i + h : 2 * i + h + 1], (SUB, rank))
                        for h in range(PACK // SUB)
                    ],
                    axis=0,
                )

            c = spread(cos_tab)
            s = spread(sin_tab)
            phased[k, rows, :rank] = (real * c + imag * s).astype(jnp.bfloat16)
            phased[k, rows, rank:] = (imag * c - real * s).astype(jnp.bfloat16)
        part = jnp.dot(left[...], phased[k], preferred_element_type=jnp.float32)

        @pl.when(color == 0)
        def _():
            total[k] = part

        @pl.when(color > 0)
        def _():
            total[k] = total[k] + part

    @pl.when(color == pl.num_programs(0) - 1)
    def _():
        odd = place_ref[1] == 1
        for k in range(count):
            re = (total[k, :rank, :rank] + total[k, rank:, rank:]) * scale
            im = (total[k, :rank, rank:] - total[k, rank:, :rank]) * scale
            keep_ref[k] = jnp.where(odd, im, re)
            send_ref[k] = jnp.where(odd, re, im)


def elementals(momenta, place, vectors, first, count, extent_x, scale):
    _, colors, sites, rank = vectors.shape
    out = jax.ShapeDtypeStruct((count, rank, rank), jnp.float32)
    smem = pl.BlockSpec(memory_space=pltpu.SMEM)
    return pl.pallas_call(
        functools.partial(elemental_kernel, first, count, extent_x, scale),
        grid=(colors,),
        in_specs=[smem, smem, pl.BlockSpec((2, 1, sites, rank), lambda c: (0, c, 0, 0))],
        out_specs=[pl.BlockSpec(memory_space=pltpu.VMEM)] * 2,
        out_shape=[out, out],
        scratch_shapes=[
            pltpu.VMEM((2 * rank, sites), jnp.bfloat16),
            pltpu.VMEM((count, sites, 2 * rank), jnp.bfloat16),
            pltpu.VMEM((count, 2 * rank, 2 * rank), jnp.float32),
        ],
        name="elementals",
    )(momenta, place, vectors)


def split_two(x):
    high = x.astype(jnp.bfloat16)
    return high, (x - high.astype(jnp.float32)).astype(jnp.bfloat16)


def bdot(a, b):
    return jnp.dot(a, b, preferred_element_type=jnp.float32)


def sink_kernel(spins, place_ref, mom_ref, pick_ref, mine0, other0, mine1, other1, per_ref, high_ref, low_ref):
    rank = per_ref.shape[-1]
    odd = place_ref[1] == 1
    start = place_ref[2]
    for j in range(spins):
        m = mom_ref[start + j]
        q = pick_ref[start + j]
        rest = jnp.maximum(m - 1, 0)
        mine = jnp.where(m == 0, mine0[0], mine1[rest])
        other = jnp.where(m == 0, other0[0], other1[rest])
        re_h, re_l = split_two(jnp.where(odd, other, mine))
        im_h, im_l = split_two(jnp.where(odd, mine, other))
        weights = jnp.concatenate([per_ref[q, 0], per_ref[q, 1]], axis=1)
        from_re = bdot(re_h, weights) + bdot(re_l, weights)
        from_im = bdot(im_h, weights) + bdot(im_l, weights)
        out_re = from_re[:, :rank] - from_im[:, rank:]
        out_im = from_re[:, rank:] + from_im[:, :rank]
        high_ref[j, 0], low_ref[j, 0] = split_two(out_re)
        high_ref[j, 1], low_ref[j, 1] = split_two(out_im)


def corr_kernel(scale, place_ref, high_ref, low_ref, mine_ref, other_ref, out_ref):
    spins, _, rank, _ = high_ref.shape
    odd = place_ref[1] == 1
    mine = mine_ref[0]
    other = other_ref[0]
    re_h, re_l = split_two(jnp.where(odd, other, mine))
    im_h, im_l = split_two(jnp.where(odd, mine, other))
    w_h = jnp.concatenate([re_h, im_h], axis=1)
    w_l = jnp.concatenate([re_l, im_l], axis=1)
    for j in range(spins):
        high = high_ref[j].reshape(2 * rank, rank)
        low = low_ref[j].reshape(2 * rank, rank)
        full = bdot(high, w_h) + (bdot(high, w_l) + bdot(low, w_h))
        out_ref[0, j, 0] = (full[:rank, :rank] - full[rank:, rank:]) * scale
        out_ref[0, j, 1] = (full[:rank, rank:] + full[rank:, :rank]) * scale


def swap(array, axis, bit):
    return lax.ppermute(array, axis, [(i, i ^ bit) for i in range(lax.axis_size(axis))])


def bits(size):
    return [1 << k for k in range((size - 1).bit_length())]


def chip_sum(keep, send):
    total = keep + swap(send, "gx", 1)
    for bit in bits(lax.axis_size("gx"))[1:]:
        total = total + swap(total, "gx", bit)
    return total


def body(vectors, peramb, momenta, sink_mom, spin_pick, src_time):
    vectors = vectors[0]
    peramb = peramb[0]
    _, colors, sites, rank = vectors.shape
    groups = lax.axis_size("gx")
    slab_x = sites // (LY * LZ)
    extent_x = slab_x * groups
    me = lax.axis_index("gx")
    spins = sink_mom.shape[0] // groups
    place = jnp.stack([me * slab_x, me % 2, me * spins]).astype(jnp.int32)
    scale = 1.0 / math.sqrt(colors * sites * groups)
    count = momenta.shape[0]
    run = functools.partial(
        elementals, momenta, place, vectors, extent_x=extent_x, scale=scale
    )
    slices = lax.axis_size("ta")
    root = jnp.mod(src_time[0], slices)
    apart = jnp.bitwise_xor(root, lax.axis_index("ta"))

    mine0 = chip_sum(*run(first=0, count=1))
    mine1 = chip_sum(*run(first=1, count=count - 1))
    source = mine0
    for bit in bits(slices):
        source = jnp.where(jnp.bitwise_and(apart, bit) != 0, swap(source, "ta", bit), source)
    source_other = swap(source, "gx", 1)
    other0 = swap(mine0, "gx", 1)
    other1 = swap(mine1, "gx", 1)

    smem = pl.BlockSpec(memory_space=pltpu.SMEM)
    vmem = pl.BlockSpec(memory_space=pltpu.VMEM)
    pair = jax.ShapeDtypeStruct((spins, 2, rank, rank), jnp.bfloat16)
    high, low = pl.pallas_call(
        functools.partial(sink_kernel, spins),
        in_specs=[smem] * 3 + [vmem] * 5,
        out_specs=[vmem] * 2,
        out_shape=[pair, pair],
        name="sink",
    )(place, sink_mom, spin_pick, mine0, other0, mine1, other1, peramb)
    return pl.pallas_call(
        functools.partial(corr_kernel, 1.0 / math.sqrt(rank)),
        in_specs=[smem] + [vmem] * 4,
        out_specs=vmem,
        out_shape=jax.ShapeDtypeStruct((1, spins, 2, rank, rank), jnp.float32),
        name="corr",
    )(place, high, low, source, source_other)


def solution(mesh):
    placed = (
        P(("grp", "ta"), None, None, "gx", None),
        P(("grp", "ta"), None, None, None, None),
        P("grp", None),
        P("grp"),
        P("grp"),
        P("grp"),
    )
    return jax.shard_map(
        body,
        mesh=mesh,
        in_specs=placed,
        out_specs=P(("grp", "ta"), "gx", None, None, None),
        check_vma=False,
    )
```
